1024 devices in a mesh: kgrp: 64 (over x, z), scr: 16 (over y, core).
Axes of the slice: x: 8, y: 8, z: 8, core: 2. Of those that a mesh axis runs over, the one named last changes fastest.
Arguments:
- wave_val: bfloat16 [64, 32, 2048], P('kgrp', None, 'scr'), may hold values from -6 to 6
- wave_con: bfloat16 [64, 32, 2048], P('kgrp', None, 'scr'), may hold values from -6 to 6
- excite: bfloat16 [64, 1024, 16], P('kgrp', 'scr'), may hold values from -6 to 6
- screening: bfloat16 [64, 2048, 2048], P('kgrp', None, 'scr'), may hold values from -9.1552734e-05 to 9.1552734e-05
- pair_count: int32 [64], P('kgrp'), may hold values from 1 to 2, as said below
- pair_kpoint: int32 [64, 2], P('kgrp'), may hold values from 0 to 63
- pair_partner: int32 [64, 2], P('kgrp'), may hold values from 0 to 63
Outputs:
- forward: float32 [64, 2, 1024, 16], P('kgrp', None, 'scr')
- transposed: float32 [64, 2, 1024, 16], P('kgrp', None, 'scr')
The draws below stay inside these ranges and needn't reach their ends.
Inputs may be any that keep to these rules, and one draw needn't show every extreme that they name: Slot p of screening owner h is live when p < pair_count[h]; in every draw some owner has 2 live slots.
All inputs are finite; a program needn't handle non-finite values.
Results may differ from the reference program's by a relative error of at most 0.0057.
Values may be sent and summed in bfloat16 or wider, within the bound.
A program may use at most 64 MiB of HBM per device.

```python
import jax
import jax.numpy as jnp
from jax import lax

NV = 32
NC = 32
NMU = 2048
PTS_BLK = 128
MAXP = 2
NEXC = 16
NPB = 1024
NK = 64
NQ = 64


def draw_pair_count(key, part):
    first_key, second_key = jax.random.split(jax.random.fold_in(key, 17))
    counts = jax.random.randint(first_key, (NQ,), 1, MAXP + 1)
    place = jax.random.randint(second_key, (), 0, NQ)
    return jnp.where(jnp.arange(NQ) == place, MAXP, counts).astype(jnp.int32)


def place_ends(entries, stream_key, least, top_value):
    spot = [jax.random.randint(jax.random.fold_in(stream_key, axis), (), 0, length) for axis, length in enumerate(entries.shape)]
    longest = entries.shape.index(max(entries.shape))
    beside = spot[:longest] + [(spot[longest] + 1) % entries.shape[longest]] + spot[longest + 1:]
    return entries.at[tuple(spot)].set(least).at[tuple(beside)].set(top_value)


def levels(key, dims, shards, least, largest):
    gain = 1.0
    for axis_at, blocks in shards:
        heights = jax.random.uniform(jax.random.fold_in(jax.random.fold_in(key, 6), axis_at), (blocks,), jnp.float32, least / len(shards), largest / len(shards))
        gain = gain * jnp.repeat(jnp.exp(heights), dims[axis_at] // blocks).reshape((-1,) + (1,) * (len(dims) - 1 - axis_at))
    return gain


def noise(key, shape, deviation, limit, pieces=(), kind=jnp.bfloat16):
    entries = deviation * jax.random.normal(key, shape, jnp.float32)
    if pieces:
        entries = entries * levels(key, shape, pieces, -0.22, 0.18)
    return jnp.clip(entries, -limit, limit).astype(kind)


def setup_inputs(seed: int = 0) -> dict:
    streams_of = jax.random.split(jax.random.key(seed), 8)
    wave_val = noise(streams_of[0], (NK, NV, NMU), 1.0, 6.0, ((0, 64), (2, 16)))
    wave_con = noise(streams_of[1], (NK, NC, NMU), 1.0, 6.0, ((0, 64), (2, 16)))
    excite = noise(streams_of[2], (NK, NPB, NEXC), 1.0, 6.0, ((0, 64), (1, 16)))
    screening = noise(streams_of[3], (NQ, NMU, NMU), (NV * NC * NMU * NMU) ** -0.5, 9.1552734375e-05, ((0, 64), (2, 16)))
    pair_count = draw_pair_count(jax.random.fold_in(streams_of[7], 71), 0)
    pair_kpoint = place_ends(jax.random.randint(streams_of[5], (NQ, MAXP), 0, NK), jax.random.fold_in(streams_of[5], 1), 0, NK - 1).astype(jnp.int32)
    pair_partner = place_ends(jax.random.randint(streams_of[6], (NQ, MAXP), 0, NK), jax.random.fold_in(streams_of[6], 1), 0, NK - 1).astype(jnp.int32)
    return dict(wave_val=wave_val, wave_con=wave_con, excite=excite, screening=screening, pair_count=pair_count, pair_kpoint=pair_kpoint, pair_partner=pair_partner)


def pair_terms(indices, wave_val, wave_con, excite, screening):
    owner = indices[0]
    first = indices[1]
    second = indices[2]
    weights = lax.dynamic_index_in_dim(screening, owner, 0, keepdims=False)
    val_first = lax.dynamic_index_in_dim(wave_val, first, 0, keepdims=False).astype(jnp.float32)
    val_second = lax.dynamic_index_in_dim(wave_val, second, 0, keepdims=False).astype(jnp.float32)
    con_first = lax.dynamic_index_in_dim(wave_con, first, 0, keepdims=False).astype(jnp.float32)
    con_second = lax.dynamic_index_in_dim(wave_con, second, 0, keepdims=False).astype(jnp.float32)
    exc_first = lax.dynamic_index_in_dim(excite, first, 0, keepdims=False).astype(jnp.float32).reshape(NV, NC, NEXC)
    exc_second = lax.dynamic_index_in_dim(excite, second, 0, keepdims=False).astype(jnp.float32).reshape(NV, NC, NEXC)
    rho_con = (con_first[:, None, :] * con_second[None, :, :]).astype(jnp.bfloat16).reshape(NC * NC, NMU)
    screened = jnp.dot(rho_con, weights, preferred_element_type=jnp.float32).astype(jnp.bfloat16)
    rho_val = (val_first.T[:, :, None] * val_second.T[:, None, :]).astype(jnp.bfloat16).reshape(NMU, NV * NV)

    def add_block(carried, block_index):
        offset = (block_index * PTS_BLK).astype(jnp.int32)
        part_screen = lax.dynamic_slice_in_dim(screened, offset, PTS_BLK, 1)
        part_val = lax.dynamic_slice_in_dim(rho_val, offset, PTS_BLK, 0)
        kernel = jnp.dot(part_screen, part_val, preferred_element_type=jnp.float32).astype(jnp.bfloat16)
        kernel = lax.optimization_barrier(kernel).astype(jnp.float32).reshape(NC, NC, NV, NV)
        ahead = carried[0] + jnp.einsum("cdvw,wde->vce", kernel, exc_second, precision=lax.Precision.HIGHEST)
        back = carried[1] + jnp.einsum("cdvw,vce->wde", kernel, exc_first, precision=lax.Precision.HIGHEST)
        return (ahead, back), None

    zeros = jnp.zeros((NV, NC, NEXC), jnp.float32)
    totals, unused = lax.scan(add_block, (zeros, zeros), jnp.arange(NMU // PTS_BLK, dtype=jnp.int32))
    return totals[0].reshape(NPB, NEXC), totals[1].reshape(NPB, NEXC)


def reference(wave_val, wave_con, excite, screening, pair_count, pair_kpoint, pair_partner):
    owners = jnp.repeat(jnp.arange(NQ, dtype=jnp.int32), MAXP)
    indices = jnp.stack([owners, pair_kpoint.reshape(-1).astype(jnp.int32), pair_partner.reshape(-1).astype(jnp.int32)], axis=1)
    ahead, back = lax.map(lambda row: pair_terms(row, wave_val, wave_con, excite, screening), indices)
    live = (jnp.arange(MAXP, dtype=jnp.int32)[None, :] < pair_count[:, None]).astype(jnp.float32)
    live = live[:, :, None, None]
    forward = ahead.reshape(NQ, MAXP, NPB, NEXC) * live
    transposed = back.reshape(NQ, MAXP, NPB, NEXC) * live
    return forward, transposed
```

```python
import math

import jax
import jax.numpy as jnp
from jax import lax
from jax.experimental import pallas as pl
from jax.experimental.pallas import tpu as pltpu
from jax.sharding import PartitionSpec as P

MESH = pl.DeviceIdType.MESH
BF16 = jnp.bfloat16
F32 = jnp.float32

NB = 32
NE = 16
PT = 128
DE = NB * NE


def ring(n):
    right, left = n // 2, (n - 1) // 2
    out = []
    for s in range(1, right + 1):
        out.append(("R", s))
        if s <= left:
            out.append(("L", s))
    return out


def slot_of(kind, s):
    return 2 * s - 1 if kind == "R" else 2 * s


def build(nx, nz, ny):
    steps_x, steps_z, steps_y = ring(nx), ring(nz), ring(ny)
    right_x, right_z = nx // 2, nz // 2

    def chunks(n):
        edges = sorted({0, min(3, n), min(5, n), n})
        return [(a, b) for a, b in zip(edges[:-1], edges[1:])]

    n_sems = 320

    def kernel(
        val_ref, con_ref, exc_ref, scr_ref, cnt_ref, first_ref, second_ref,
        fwd_ref, back_ref,
        W, GCA, GCB, GVA, GVB, GE, CB, SC, EB, SE, VB, SV, own_e,
        xt, xr, S, E32, Y1, Y2, V32, Zf, Zb, T32, SB, RB, O32,
        send_sem, recv_sem, local_sem,
    ):
        g = lax.axis_index("kgrp")
        sc = lax.axis_index("scr")
        x = lax.div(g, nz)
        z = lax.rem(g, nz)
        y = lax.div(sc, 2)
        core = lax.rem(sc, 2)
        other = 1 - core

        def at_x(d):
            return (lax.rem(x + d + nx, nx) * nz + z, sc)

        def at_z(d):
            return (x * nz + lax.rem(z + d + nz, nz), sc)

        def at_y(d):
            return (g, lax.rem(y + d + ny, ny) * 2 + core)

        partner = (g, y * 2 + other)

        peers = [partner]
        for n, at in ((nx, at_x), (nz, at_z), (ny, at_y)):
            if n > 2:
                peers += [at(1), at(-1)]
            elif n == 2:
                peers += [at(1)]
        barrier = pltpu.get_barrier_semaphore()
        for peer in peers:
            pl.semaphore_signal(barrier, inc=1, device_id=peer, device_id_type=MESH)
        pl.semaphore_wait(barrier, len(peers))

        started = []
        count = [0]

        def send(src, dst, to):
            k = count[0]
            count[0] += 1
            copy = pltpu.make_async_remote_copy(
                src_ref=src, dst_ref=dst, send_sem=send_sem.at[k], recv_sem=recv_sem.at[k],
                device_id=to, device_id_type=MESH,
            )
            copy.start()
            started.append(copy)
            return copy

        class Ring:
            def __init__(self, n, at, view, own=None):
                self.n, self.at, self.view = n, at, view
                self.right, self.left = n // 2, (n - 1) // 2
                self.flight = {}
                self.own = own

            def begin(self):
                for kind, d, last in (("R", 1, self.right), ("L", -1, self.left)):
                    if last >= 1:
                        src = self.view(0) if self.own is None else self.own
                        self.flight[kind, 1] = send(src, self.view(slot_of(kind, 1)), self.at(d))

            def step(self, s):
                for kind, d, last in (("R", 1, self.right), ("L", -1, self.left)):
                    if s <= last:
                        self.flight[kind, s].wait_recv()
                        if s + 1 <= last:
                            self.flight[kind, s + 1] = send(
                                self.view(slot_of(kind, s)), self.view(slot_of(kind, s + 1)), self.at(d)
                            )

        ca1 = Ring(nx, at_x, lambda k: GCA.at[0, k], con_ref.at[pl.ds(0, 16)])
        cb1 = Ring(nz, at_z, lambda k: GCB.at[0, k], con_ref.at[pl.ds(16, 16)])
        ca1.begin()
        cb1.begin()
        w_here = pltpu.make_async_copy(scr_ref, W.at[core], local_sem)
        w_here.start()
        xt[...] = jnp.zeros_like(xt)
        xr[...] = jnp.zeros_like(xr)
        xt[:, 0:64] = exc_ref[...].astype(F32)
        xr[:, 0:NE] = xt[...].T[:, 0:NE]
        packed = xr[pl.ds(0, 8, stride=8), :]
        for k in range(1, 8):
            packed = packed + pltpu.roll(xr[pl.ds(k, 8, stride=8), :], NE * k, 1)
        own_e[...] = packed.astype(BF16)
        GE[0, 0] = packed.astype(BF16)
        GCA[0, 0] = con_ref[0:16, :]
        GCB[0, 0] = con_ref[16:32, :]
        GVA[0, 0] = val_ref[0:16, :]
        GVB[0, 0] = val_ref[16:32, :]
        va1 = Ring(nx, at_x, lambda k: GVA.at[0, k], val_ref.at[pl.ds(0, 16)])
        vb1 = Ring(nz, at_z, lambda k: GVB.at[0, k], val_ref.at[pl.ds(16, 16)])
        ex1 = Ring(nx, at_x, lambda k: GE.at[0, k], own_e)
        ex1.begin()
        va1.begin()
        vb1.begin()
        w_there = send(scr_ref, W.at[core], partner)

        def second(buf, n_first, n, at, lo, hi):
            return Ring(n, at, lambda k: buf.at[k, pl.ds(lo, hi - lo)])

        con_rings = []
        for lo, hi in chunks(nx):
            con_rings.append((hi // 2, second(GCA, nx, nz, at_z, lo, hi)))
        for lo, hi in chunks(nz):
            con_rings.append((hi // 2, second(GCB, nz, nx, at_x, lo, hi)))
        ex2 = second(GE, nx, nz, at_z, 0, nx)
        va2 = second(GVA, nx, nz, at_z, 0, nx)
        vb2 = second(GVB, nz, nx, at_x, 0, nz)
        half = max(nx, nz) // 2
        for t in range(1, 2 * half + 1):
            ca1.step(t)
            cb1.step(t)
            for ready, r in con_rings:
                if t == ready:
                    r.begin()
                elif t > ready:
                    r.step(t - ready)
            ex1.step(t)
            if t == half:
                ex2.begin()
            elif t > half:
                ex2.step(t - half)
            va1.step(t)
            vb1.step(t)
            if t == half:
                va2.begin()
                vb2.begin()

        def slots(k):
            kx = lax.div(k, nz)
            kz = lax.rem(k, nz)
            rx = lax.rem(x - kx + nx, nx)
            rz = lax.rem(z - kz + nz, nz)
            sx = jnp.where(rx <= right_x, jnp.maximum(2 * rx - 1, 0), 2 * (nx - rx))
            sz = jnp.where(rz <= right_z, jnp.maximum(2 * rz - 1, 0), 2 * (nz - rz))
            return sx, sz

        chosen = {}
        for name, p in (("own", core), ("other", other)):
            for role, ref in ((0, first_ref), (1, second_ref)):
                chosen[name, role] = slots(ref[0, p])

        for role in (0, 1):
            sx, sz = chosen["other", role]
            SC[role, 0:16, :] = GCA[sz, sx]
            SC[role, 16:32, :] = GCB[sx, sz]
            sx, sz = chosen["own", role]
            CB[0, core, role, 0:16, :] = GCA[sz, sx]
            CB[0, core, role, 16:32, :] = GCB[sx, sz]
        for role in (0, 1):
            sx, sz = chosen["other", role]
            SE[role] = GE[sz, sx]
            sx, sz = chosen["own", role]
            EB[0, core, role] = GE[sz, sx]
        pc = send(SC, CB.at[0, core], partner)
        y_own = Ring(ny, at_y, lambda k: CB.at[k, core])
        y_oth = Ring(ny, at_y, lambda k: CB.at[k, other])
        y_exc = Ring(ny, at_y, lambda k: EB.at[k])
        y_own.begin()
        pe = send(SE, EB.at[0, core], partner)
        pc.wait_recv()
        y_oth.begin()
        pe.wait_recv()
        y_exc.begin()
        w_here.wait()
        w_there.wait_recv()

        def y_from(k):
            if k == 0:
                return y
            s = (k + 1) // 2
            return lax.rem(y - s + ny, ny) if k % 2 == 1 else lax.rem(y + s, ny)

        def block(k):
            row = pl.multiple_of(y_from(k) * (2 * PT), 2 * PT)
            w = jnp.concatenate([W[0, pl.ds(row, 2 * PT), :], W[1, pl.ds(row, 2 * PT), :]], axis=1)
            c1 = jnp.concatenate([CB[k, 0, 0], CB[k, 1, 0]], axis=1).astype(F32)
            c2 = jnp.concatenate([CB[k, 0, 1], CB[k, 1, 1]], axis=1).astype(F32)
            for b in range(4):
                rho = jnp.concatenate(
                    [(c1[c : c + 1, :] * c2).astype(BF16) for c in range(8 * b, 8 * b + 8)], axis=0
                )
                part = jnp.dot(rho, w, preferred_element_type=F32)
                for lane in range(2):
                    piece = part[:, 128 * lane : 128 * lane + 128]
                    if k == 0:
                        S[lane, pl.ds(256 * b, 256), :] = piece
                    else:
                        S[lane, pl.ds(256 * b, 256), :] += piece

        block(0)
        for t in range(1, max(half, ny // 2) + 1):
            y_own.step(t)
            y_oth.step(t)
            y_exc.step(t)
            va2.step(t)
            vb2.step(t)
            for kind, s in steps_y:
                if s == t:
                    block(slot_of(kind, s))

        for role in (0, 1):
            sx, sz = chosen["other", role]
            SV[role, 0:16, :] = GVA[sz, sx]
            SV[role, 16:32, :] = GVB[sx, sz]
            sx, sz = chosen["own", role]
            VB[core, role, 0:16, :] = GVA[sz, sx]
            VB[core, role, 16:32, :] = GVB[sx, sz]
        pv = send(SV, VB.at[core], partner)

        for k in range(ny):
            for c in range(2):
                row = pl.multiple_of((y_from(k) * 2 + c) * 8, 8)
                for role in (0, 1):
                    E32[role, pl.ds(row, 8), :] = EB[k, c, role].astype(F32)
        pv.wait_recv()
        vals = [jnp.concatenate([VB[0, role], VB[1, role]], axis=1) for role in (0, 1)]
        nw = 4 * ny
        for role, out in ((0, Y1), (1, Y2)):
            for lane in range(2):
                V32[role, lane] = VB[lane, role].astype(F32)
            for q in range(4):
                eq = E32[role, pl.ds(q, nw, stride=4), :].astype(BF16)
                out[pl.ds(q * 128, 128), :] = lax.dot_general(
                    eq, vals[role][0:nw], (((0,), (0,)), ((), ())), preferred_element_type=F32
                )
        Zb[...] = jnp.zeros_like(Zb)

        def z_block(i, carry):
            for lane in range(2):
                cols = pl.ds(lane * 128, 128)
                y1 = [Y1[pl.ds(pl.multiple_of((i * 8 + c) * NE, NE), NE), cols] for c in range(8)]

                def over_d(d, acc):
                    at = pl.multiple_of(d * NE, NE)
                    y2 = Y2[pl.ds(at, NE), cols]
                    mirror = pl.multiple_of((d + 7 - 2 * lax.rem(d, 8)) * NE, NE)
                    zb = Zb[pl.ds(mirror, NE), cols]
                    new = []
                    for c in range(8):
                        s = S[lane, pl.ds((i * 8 + c) * NB + d, 1), :]
                        new.append(acc[c] + s * y2)
                        zb = zb + s * y1[c]
                    Zb[pl.ds(mirror, NE), cols] = zb
                    return tuple(new)

                zero = tuple(jnp.zeros((NE, 128), F32) for c in range(8))
                acc = lax.fori_loop(0, NB, over_d, zero)
                for c in range(8):
                    Zf[pl.ds(pl.multiple_of((i * 8 + 7 - c) * NE, NE), NE), cols] = acc[c]
            return carry

        lax.fori_loop(0, 4, z_block, 0)

        for fb, Z, role in ((0, Zf, 0), (1, Zb, 1)):
            v = jnp.concatenate(
                [
                    jnp.concatenate(
                        [V32[role, lane, pl.ds(i, 16, stride=2), :] for lane in range(2)], axis=1
                    )
                    for i in range(2)
                ],
                axis=0,
            ).astype(BF16)
            for h in range(4):
                f = lax.dot_general(
                    v, Z[pl.ds(h * 128, 128), :].astype(BF16), (((1,), (1,)), ((), ())),
                    preferred_element_type=F32,
                )
                for i in range(2):
                    T32[pl.ds(fb * 8 + h * 2 + i, 16, stride=16), :] = f[16 * i : 16 * i + 16, :]
        n_scr = 2 * ny
        for s in range(n_scr):
            SB[s] = T32[pl.ds(16 * s, 16), :].astype(BF16)
        RB[core, 0] = SB[sc]
        sums = []
        for d in range(ny):
            for c, cc in ((0, core), (1, other)):
                if d == 0 and c == 0:
                    continue
                yy = lax.rem(y + d, ny)
                to = yy * 2 + cc
                sums.append(send(SB.at[to], RB.at[core, d], (g, to)))
        for copy in started:
            copy.wait_send()
        for copy in sums:
            copy.wait_recv()
        O32[...] = jnp.zeros_like(O32)
        for p in range(2):
            live = jnp.where(p < cnt_ref[0], 1.0, 0.0).astype(F32)
            tot = RB[p, 0].astype(F32)
            for d in range(1, ny):
                tot = tot + RB[p, d].astype(F32)
            tot = tot * live
            for fb, out in ((0, fwd_ref), (1, back_ref)):
                for i in range(2):
                    for h in range(4):
                        r = fb * 8 + h * 2 + i
                        row = jnp.broadcast_to(tot[r : r + 1, :], (8, 128))
                        O32[pl.ds(i * 32 + h * 8, 8), :] = pltpu.roll(
                            pltpu.roll(row, NE, 1), 0, 1, stride=NE, stride_axis=0
                        )
                out[p] = O32[...].T[0:NE, 0:64]

    def run(wave_val, wave_con, excite, screening, pair_count, pair_kpoint, pair_partner):
        vmem = pl.BlockSpec(memory_space=pltpu.VMEM)
        smem = pl.BlockSpec(memory_space=pltpu.SMEM)
        n_mu = 2 * PT * ny
        shape = jax.ShapeDtypeStruct((2, NE, 64), F32)
        V = pltpu.VMEM
        fwd, back = pl.pallas_call(
            kernel,
            out_shape=(shape, shape),
            in_specs=[vmem, vmem, vmem, pl.BlockSpec(memory_space=pl.ANY), smem, smem, smem],
            out_specs=(vmem, vmem),
            scratch_shapes=[
                V((2, n_mu, PT), BF16),
                V((nz, nx, 16, PT), BF16), V((nx, nz, 16, PT), BF16),
                V((nz, nx, 16, PT), BF16), V((nx, nz, 16, PT), BF16),
                V((nz, nx, 8, PT), BF16),
                V((ny, 2, 2, NB, PT), BF16), V((2, NB, PT), BF16),
                V((ny, 2, 2, 8, PT), BF16), V((2, 8, PT), BF16),
                V((2, 2, NB, PT), BF16), V((2, NB, PT), BF16),
                V((8, PT), BF16),
                V((16, 128), F32), V((128, 128), F32),
                V((2, NB * NB, PT), F32),
                V((2, 16 * ny, 128), F32),
                V((DE, 2 * PT), F32), V((DE, 2 * PT), F32),
                V((2, 2, NB, PT), F32),
                V((DE, 2 * PT), F32), V((DE, 2 * PT), F32),
                V((256, 128), F32), V((16, 16, 128), BF16), V((2, ny, 16, 128), BF16),
                V((128, 128), F32),
                pltpu.SemaphoreType.DMA((n_sems,)), pltpu.SemaphoreType.DMA((n_sems,)),
                pltpu.SemaphoreType.DMA,
            ],
            compiler_params=pltpu.CompilerParams(
                collective_id=0, has_side_effects=True, vmem_limit_bytes=32 * 1024 * 1024
            ),
        )(
            wave_val[0], wave_con[0], jnp.transpose(excite[0]), screening[0],
            pair_count, pair_kpoint, pair_partner,
        )
        return jnp.swapaxes(fwd, 1, 2)[None], jnp.swapaxes(back, 1, 2)[None]

    return run


def solution(mesh, sides=None):
    side = math.isqrt(mesh.shape["kgrp"])
    nx, nz = sides or (side, side)
    return jax.shard_map(
        build(nx, nz, mesh.shape["scr"] // 2),
        mesh=mesh,
        in_specs=(
            P("kgrp", None, "scr"),
            P("kgrp", None, "scr"),
            P("kgrp", "scr", None),
            P("kgrp", None, "scr"),
            P("kgrp"),
            P("kgrp", None),
            P("kgrp", None),
        ),
        out_specs=(P("kgrp", None, "scr", None), P("kgrp", None, "scr", None)),
        check_vma=False,
    )
```

```python
import math

import jax
import jax.numpy as jnp
from jax import lax
from jax.experimental import pallas as pl
from jax.experimental.pallas import tpu as pltpu
from jax.sharding import PartitionSpec as P

MESH = pl.DeviceIdType.MESH
BF16 = jnp.bfloat16
F32 = jnp.float32

NB = 32
NE = 16
PT = 128
DE = NB * NE


def build(nx, nz, ny):
    n_scr = 2 * ny
    n_groups = 14 + ny

    def kernel(
        val_ref, con_ref, exc_ref, scr_ref, cnt_ref, first_ref, second_ref,
        fwd_ref, back_ref,
        W, con_v, val_v, exc_v, own_i, IX, IZ, SX, SZ,
        GCA, GCB, GVA, GVB, GE, PCA, PCB, PVA, PVB, PE, RCA, RCB, RVA, RVB, RE,
        CB, EB, xt, xr, S, E32, Y1, Y2, V32, Zf, Zb, T32, SB, RB, O32,
        send_sem, recv_sem, local_sem,
    ):
        g = lax.axis_index("kgrp")
        sc = lax.axis_index("scr")
        x = lax.div(g, nz)
        z = lax.rem(g, nz)
        y = lax.div(sc, 2)
        core = lax.rem(sc, 2)
        other = 1 - core

        def at_x(d, c):
            return (lax.rem(x + d, nx) * nz + z, y * 2 + c)

        def at_z(d, c):
            return (x * nz + lax.rem(z + d, nz), y * 2 + c)

        def at_y(d, c):
            return (g, lax.rem(y + d, ny) * 2 + c)

        def far_first(n):
            return sorted(range(1, n), key=lambda d: -min(d, n - d))

        loads = [
            pltpu.make_async_copy(src, dst, local_sem.at[i])
            for i, (src, dst) in enumerate(
                ((con_ref, con_v), (exc_ref, exc_v), (val_ref, val_v), (scr_ref, W.at[core]))
            )
        ]
        for load in loads:
            load.start()
        peers = [at_x(d, c) for d in far_first(nx) for c in (core, other)]
        peers += [at_z(d, c) for d in far_first(nz) for c in (core, other)]
        peers += [at_y(d, core) for d in far_first(ny)] + [at_y(0, other)]
        barrier = pltpu.get_barrier_semaphore()
        for peer in peers:
            pl.semaphore_signal(barrier, inc=1, device_id=peer, device_id_type=MESH)

        groups = {}

        def send(name, src, dst, to):
            k = groups.setdefault(name, len(groups))
            pltpu.make_async_remote_copy(
                src_ref=src, dst_ref=dst, send_sem=send_sem.at[k], recv_sem=recv_sem.at[k],
                device_id=to, device_id_type=MESH,
            ).start()

        def taken(name, sems, like):
            pltpu.make_async_copy(like, like, sems.at[groups[name]]).wait()

        lane = lax.broadcasted_iota(jnp.int32, (1, 128), 1)
        row = jnp.zeros((1, 128), jnp.int32)
        for i, ref in ((0, first_ref), (1, second_ref)):
            for p in range(2):
                row = jnp.where(lane == 2 * i + p, ref[0, p], row)
        own_i[...] = row
        IX[0] = row
        IZ[0] = row
        loads[0].wait()
        GCA[0] = con_v[0:16, :]
        GCB[0] = con_v[16:32, :]
        xt[...] = jnp.zeros_like(xt)
        xr[...] = jnp.zeros_like(xr)
        loads[1].wait()
        xt[:, 0:64] = exc_v[...].astype(F32)
        xr[:, 0:NE] = xt[...].T[:, 0:NE]
        packed = xr[pl.ds(0, 8, stride=8), :]
        for k in range(1, 8):
            packed = packed + pltpu.roll(xr[pl.ds(k, 8, stride=8), :], NE * k, 1)
        GE[0] = packed.astype(BF16)
        loads[2].wait()
        GVA[0] = val_v[0:16, :]
        GVB[0] = val_v[16:32, :]
        pl.semaphore_wait(barrier, len(peers))

        for d in far_first(nx):
            send("ix", own_i, IX.at[d], at_x(d, core))
        for d in far_first(nz):
            send("iz", own_i, IZ.at[d], at_z(d, core))
        for d in far_first(nx):
            send("ca1", con_v.at[pl.ds(0, 16)], GCA.at[d], at_x(d, core))
        for d in far_first(nz):
            send("cb1", con_v.at[pl.ds(16, 16)], GCB.at[d], at_z(d, core))
        for d in far_first(nx):
            send("e1", GE.at[0], GE.at[d], at_x(d, core))
        for d in far_first(nx):
            send("va1", val_v.at[pl.ds(0, 16)], GVA.at[d], at_x(d, core))
        for d in far_first(nz):
            send("vb1", val_v.at[pl.ds(16, 16)], GVB.at[d], at_z(d, core))
        send("w", scr_ref, W.at[core], at_y(0, other))

        taken("ix", recv_sem, IX.at[pl.ds(0, nx - 1)])
        ix_down = pltpu.make_async_copy(IX, SX, local_sem.at[0])
        ix_down.start()
        taken("iz", recv_sem, IZ.at[pl.ds(0, nz - 1)])
        iz_down = pltpu.make_async_copy(IZ, SZ, local_sem.at[1])
        iz_down.start()

        def place(k, here, n, of):
            return lax.rem(here - of(k) + n, n)

        def kx_of(k):
            return lax.div(k, nz)

        def kz_of(k):
            return lax.rem(k, nz)

        iz_down.wait()
        ix_down.wait()
        from_x = {}
        from_z = {}
        for p in range(2):
            for r in range(2):
                for d in range(nz):
                    from_x[d, p, r] = place(SZ[(nz - d) % nz, 0, 2 * r + p], x, nx, kx_of)
                for d in range(nx):
                    from_z[d, p, r] = place(SX[(nx - d) % nx, 0, 2 * r + p], z, nz, kz_of)

        def hand_on(name, held, packed, landed, where, n, at):
            order = far_first(n) + [0]
            for d in order:
                for p in range(2):
                    for r in range(2):
                        packed[2 * d + p, r] = held[where[d, p, r]]
            for d in order[:-1]:
                for p in range(2):
                    send(name, packed.at[2 * d + p], landed.at[2 * d + core], at(d, p))
            send(name, packed.at[other], landed.at[core], at(0, other))
            landed[core] = packed[core]

        taken("ca1", recv_sem, GCA.at[pl.ds(0, nx - 1)])
        hand_on("ca2", GCA, PCA, RCA, from_x, nz, at_z)
        taken("cb1", recv_sem, GCB.at[pl.ds(0, nz - 1)])
        hand_on("cb2", GCB, PCB, RCB, from_z, nx, at_x)
        taken("e1", recv_sem, GE.at[pl.ds(0, nx - 1)])
        hand_on("e2", GE, PE, RE, from_x, nz, at_z)
        taken("va1", recv_sem, GVA.at[pl.ds(0, nx - 1)])
        hand_on("va2", GVA, PVA, RVA, from_x, nz, at_z)
        taken("vb1", recv_sem, GVB.at[pl.ds(0, nz - 1)])
        hand_on("vb2", GVB, PVB, RVB, from_z, nx, at_x)

        mine = []
        for ref in (first_ref, second_ref):
            k = ref[0, core]
            mine.append((place(k, z, nz, kz_of), place(k, x, nx, kx_of)))

        taken("ca2", recv_sem, RCA.at[pl.ds(0, 2 * nz - 1)])
        for r in range(2):
            for c in range(2):
                CB[0, c, r, 0:16, :] = RCA[2 * mine[r][0] + c, r]
        taken("cb2", recv_sem, RCB.at[pl.ds(0, 2 * nx - 1)])
        for r in range(2):
            for c in range(2):
                CB[0, c, r, 16:32, :] = RCB[2 * mine[r][1] + c, r]
        for d in far_first(ny):
            send(f"y{d}", CB.at[0], CB.at[d], at_y(d, core))
        taken("e2", recv_sem, RE.at[pl.ds(0, 2 * nz - 1)])
        for r in range(2):
            for c in range(2):
                EB[0, c, r] = RE[2 * mine[r][0] + c, r]
        for d in far_first(ny):
            send("ye", EB.at[0], EB.at[d], at_y(d, core))
        loads[3].wait()
        taken("w", recv_sem, W.at[0])

        def y_from(k):
            return lax.rem(y - k + ny, ny)

        def block(k):
            row = pl.multiple_of(y_from(k) * (2 * PT), 2 * PT)
            w = jnp.concatenate([W[0, pl.ds(row, 2 * PT), :], W[1, pl.ds(row, 2 * PT), :]], axis=1)
            c1 = jnp.concatenate([CB[k, 0, 0], CB[k, 1, 0]], axis=1).astype(F32)
            c2 = jnp.concatenate([CB[k, 0, 1], CB[k, 1, 1]], axis=1).astype(F32)
            for b in range(4):
                rho = jnp.concatenate(
                    [(c1[c : c + 1, :] * c2).astype(BF16) for c in range(8 * b, 8 * b + 8)], axis=0
                )
                part = jnp.dot(rho, w, preferred_element_type=F32)
                for lane in range(2):
                    piece = part[:, 128 * lane : 128 * lane + 128]
                    if k == 0:
                        S[lane, pl.ds(256 * b, 256), :] = piece
                    else:
                        S[lane, pl.ds(256 * b, 256), :] += piece

        block(0)
        near_first = sorted(range(1, ny), key=lambda d: (min(d, ny - d), d))
        for d in near_first:
            taken(f"y{d}", recv_sem, CB.at[0])
            block(d)
        taken("va2", recv_sem, RVA.at[pl.ds(0, 2 * nz - 1)])
        taken("vb2", recv_sem, RVB.at[pl.ds(0, 2 * nx - 1)])
        vals = []
        for r in range(2):
            halves = []
            for c in range(2):
                top = RVA[2 * mine[r][0] + c, r]
                low = RVB[2 * mine[r][1] + c, r]
                both = jnp.concatenate([top, low], axis=0)
                V32[r, c] = both.astype(F32)
                halves.append(both)
            vals.append(jnp.concatenate(halves, axis=1))
        taken("ye", recv_sem, EB.at[pl.ds(0, ny - 1)])
        for k in range(ny):
            for c in range(2):
                row = pl.multiple_of((y_from(k) * 2 + c) * 8, 8)
                for role in (0, 1):
                    E32[role, pl.ds(row, 8), :] = EB[k, c, role].astype(F32)
        nw = 4 * ny
        for role, out in ((0, Y1), (1, Y2)):
            for q in range(4):
                eq = E32[role, pl.ds(q, nw, stride=4), :].astype(BF16)
                out[pl.ds(q * 128, 128), :] = lax.dot_general(
                    eq, vals[role][0:nw], (((0,), (0,)), ((), ())), preferred_element_type=F32
                )
        Zb[...] = jnp.zeros_like(Zb)

        def z_block(i, carry):
            for lane in range(2):
                cols = pl.ds(lane * 128, 128)
                y1 = [Y1[pl.ds(pl.multiple_of((i * 8 + c) * NE, NE), NE), cols] for c in range(8)]

                def over_d(d, acc):
                    at = pl.multiple_of(d * NE, NE)
                    y2 = Y2[pl.ds(at, NE), cols]
                    mirror = pl.multiple_of((d + 7 - 2 * lax.rem(d, 8)) * NE, NE)
                    zb = Zb[pl.ds(mirror, NE), cols]
                    new = []
                    for c in range(8):
                        s = S[lane, pl.ds((i * 8 + c) * NB + d, 1), :]
                        new.append(acc[c] + s * y2)
                        zb = zb + s * y1[c]
                    Zb[pl.ds(mirror, NE), cols] = zb
                    return tuple(new)

                zero = tuple(jnp.zeros((NE, 128), F32) for c in range(8))
                acc = lax.fori_loop(0, NB, over_d, zero)
                for c in range(8):
                    Zf[pl.ds(pl.multiple_of((i * 8 + 7 - c) * NE, NE), NE), cols] = acc[c]
            return carry

        lax.fori_loop(0, 4, z_block, 0)

        for fb, Z, role in ((0, Zf, 0), (1, Zb, 1)):
            v = jnp.concatenate(
                [
                    jnp.concatenate(
                        [V32[role, lane, pl.ds(i, 16, stride=2), :] for lane in range(2)], axis=1
                    )
                    for i in range(2)
                ],
                axis=0,
            ).astype(BF16)
            for h in range(4):
                f = lax.dot_general(
                    v, Z[pl.ds(h * 128, 128), :].astype(BF16), (((1,), (1,)), ((), ())),
                    preferred_element_type=F32,
                )
                for i in range(2):
                    T32[pl.ds(fb * 8 + h * 2 + i, 16, stride=16), :] = f[16 * i : 16 * i + 16, :]
        for s in range(n_scr):
            SB[s] = T32[pl.ds(16 * s, 16), :].astype(BF16)
        for d in far_first(ny) + [0]:
            for c in (core, other):
                to = lax.rem(y + d, ny) * 2 + c
                if d > 0 or c is other:
                    send("sum", SB.at[to], RB.at[core * ny + d], (g, to))
        RB[core * ny] = SB[sc]
        for name, like in (
            ("ix", IX.at[pl.ds(0, nx - 1)]), ("iz", IZ.at[pl.ds(0, nz - 1)]),
            ("ca1", GCA.at[pl.ds(0, nx - 1)]), ("cb1", GCB.at[pl.ds(0, nz - 1)]),
            ("e1", GE.at[pl.ds(0, nx - 1)]),
            ("va1", GVA.at[pl.ds(0, nx - 1)]), ("vb1", GVB.at[pl.ds(0, nz - 1)]),
            ("w", W.at[0]),
            ("ca2", RCA.at[pl.ds(0, 2 * nz - 1)]), ("cb2", RCB.at[pl.ds(0, 2 * nx - 1)]),
            ("e2", RE.at[pl.ds(0, 2 * nz - 1)]),
            ("va2", RVA.at[pl.ds(0, 2 * nz - 1)]), ("vb2", RVB.at[pl.ds(0, 2 * nx - 1)]),
            ("ye", EB.at[pl.ds(0, ny - 1)]), ("sum", RB.at[pl.ds(0, n_scr - 1)]),
        ):
            taken(name, send_sem, like)
        for d in range(1, ny):
            taken(f"y{d}", send_sem, CB.at[0])
        taken("sum", recv_sem, RB.at[pl.ds(0, n_scr - 1)])
        O32[...] = jnp.zeros_like(O32)
        for p in range(2):
            live = jnp.where(p < cnt_ref[0], 1.0, 0.0).astype(F32)
            tot = RB[p * ny].astype(F32)
            for d in range(1, ny):
                tot = tot + RB[p * ny + d].astype(F32)
            tot = tot * live
            for fb, out in ((0, fwd_ref), (1, back_ref)):
                for i in range(2):
                    for h in range(4):
                        r = fb * 8 + h * 2 + i
                        row = jnp.broadcast_to(tot[r : r + 1, :], (8, 128))
                        O32[pl.ds(i * 32 + h * 8, 8), :] = pltpu.roll(
                            pltpu.roll(row, NE, 1), 0, 1, stride=NE, stride_axis=0
                        )
                out[p] = O32[...].T[0:NE, 0:64]

    def run(wave_val, wave_con, excite, screening, pair_count, pair_kpoint, pair_partner):
        vmem = pl.BlockSpec(memory_space=pltpu.VMEM)
        smem = pl.BlockSpec(memory_space=pltpu.SMEM)
        hbm = pl.BlockSpec(memory_space=pl.ANY)
        n_mu = 2 * PT * ny
        shape = jax.ShapeDtypeStruct((2, NE, 64), F32)
        V = pltpu.VMEM
        fwd, back = pl.pallas_call(
            kernel,
            out_shape=(shape, shape),
            in_specs=[hbm, hbm, hbm, hbm, smem, smem, smem],
            out_specs=(vmem, vmem),
            scratch_shapes=[
                V((2, n_mu, PT), BF16),
                V((NB, PT), BF16), V((NB, PT), BF16), V((NE, 64), BF16),
                V((1, 128), jnp.int32), V((nx, 1, 128), jnp.int32), V((nz, 1, 128), jnp.int32),
                pltpu.SMEM((nx, 1, 128), jnp.int32), pltpu.SMEM((nz, 1, 128), jnp.int32),
                V((nx, 16, PT), BF16), V((nz, 16, PT), BF16),
                V((nx, 16, PT), BF16), V((nz, 16, PT), BF16), V((nx, 8, PT), BF16),
                V((2 * nz, 2, 16, PT), BF16), V((2 * nx, 2, 16, PT), BF16),
                V((2 * nz, 2, 16, PT), BF16), V((2 * nx, 2, 16, PT), BF16), V((2 * nz, 2, 8, PT), BF16),
                V((2 * nz, 2, 16, PT), BF16), V((2 * nx, 2, 16, PT), BF16),
                V((2 * nz, 2, 16, PT), BF16), V((2 * nx, 2, 16, PT), BF16), V((2 * nz, 2, 8, PT), BF16),
                V((ny, 2, 2, NB, PT), BF16), V((ny, 2, 2, 8, PT), BF16),
                V((16, 128), F32), V((128, 128), F32),
                V((2, NB * NB, PT), F32),
                V((2, 16 * ny, 128), F32),
                V((DE, 2 * PT), F32), V((DE, 2 * PT), F32),
                V((2, 2, NB, PT), F32),
                V((DE, 2 * PT), F32), V((DE, 2 * PT), F32),
                V((256, 128), F32), V((16, 16, 128), BF16), V((n_scr, 16, 128), BF16),
                V((128, 128), F32),
                pltpu.SemaphoreType.DMA((n_groups,)), pltpu.SemaphoreType.DMA((n_groups,)),
                pltpu.SemaphoreType.DMA((4,)),
            ],
            compiler_params=pltpu.CompilerParams(
                collective_id=0, has_side_effects=True, vmem_limit_bytes=60 * 1024 * 1024
            ),
        )(
            wave_val[0], wave_con[0], jnp.transpose(excite[0]), screening[0],
            pair_count, pair_kpoint, pair_partner,
        )
        return jnp.swapaxes(fwd, 1, 2)[None], jnp.swapaxes(back, 1, 2)[None]

    return run


def solution(mesh, sides=None):
    side = math.isqrt(mesh.shape["kgrp"])
    nx, nz = sides or (side, side)
    return jax.shard_map(
        build(nx, nz, mesh.shape["scr"] // 2),
        mesh=mesh,
        in_specs=(
            P("kgrp", None, "scr"),
            P("kgrp", None, "scr"),
            P("kgrp", "scr", None),
            P("kgrp", None, "scr"),
            P("kgrp"),
            P("kgrp", None),
            P("kgrp", None),
        ),
        out_specs=(P("kgrp", None, "scr", None), P("kgrp", None, "scr", None)),
        check_vma=False,
    )
```

```python
import math

import jax
import jax.numpy as jnp
from jax import lax
from jax.experimental import pallas as pl
from jax.experimental.pallas import tpu as pltpu
from jax.sharding import PartitionSpec as P

MESH = pl.DeviceIdType.MESH
BF16 = jnp.bfloat16
F32 = jnp.float32

NB = 32
NE = 16
PT = 128
DE = NB * NE


def build(nx, nz, ny):
    n_scr = 2 * ny
    n_groups = 8 + 10 + 3 * ny + 1

    def kernel(
        val_ref, con_ref, exc_ref, scr_ref, cnt_ref, first_ref, second_ref,
        fwd_ref, back_ref,
        W, con_v, val_v, exc_v, own_i, IX, IZ, SX, SZ,
        GCA, GCB, GVA, GVB, GE, PCA, PCB, PVA, PVB, PE, RCA0, RCA1, RCB0, RCB1, RVA0, RVA1, RVB0, RVB1, RE0, RE1,
        CB, EB, xt, xr, S, E32, Y1, Y2, V32, Zf, Zb, T32, SB, RB, O32,
        send_sem, recv_sem, local_sem,
    ):
        g = lax.axis_index("kgrp")
        sc = lax.axis_index("scr")
        x = lax.div(g, nz)
        z = lax.rem(g, nz)
        y = lax.div(sc, 2)
        core = lax.rem(sc, 2)
        other = 1 - core

        def at_x(d, c):
            return (lax.rem(x + d, nx) * nz + z, y * 2 + c)

        def at_z(d, c):
            return (x * nz + lax.rem(z + d, nz), y * 2 + c)

        def at_y(d, c):
            return (g, lax.rem(y + d, ny) * 2 + c)

        def far_first(n):
            return sorted(range(1, n), key=lambda d: -min(d, n - d))

        RCA, RCB, RVA, RVB, RE = (RCA0, RCA1), (RCB0, RCB1), (RVA0, RVA1), (RVB0, RVB1), (RE0, RE1)

        loads = [
            pltpu.make_async_copy(src, dst, local_sem.at[i])
            for i, (src, dst) in enumerate(
                ((con_ref, con_v), (exc_ref, exc_v), (val_ref, val_v), (scr_ref, W.at[core]))
            )
        ]
        for load in loads:
            load.start()
        peers = [at_x(d, c) for d in far_first(nx) for c in (core, other)]
        peers += [at_z(d, c) for d in far_first(nz) for c in (core, other)]
        peers += [at_y(d, core) for d in far_first(ny)] + [at_y(0, other)]
        barrier = pltpu.get_barrier_semaphore()
        for peer in peers:
            pl.semaphore_signal(barrier, inc=1, device_id=peer, device_id_type=MESH)

        groups = {}

        def send(name, src, dst, to):
            k = groups.setdefault(name, len(groups))
            pltpu.make_async_remote_copy(
                src_ref=src, dst_ref=dst, send_sem=send_sem.at[k], recv_sem=recv_sem.at[k],
                device_id=to, device_id_type=MESH,
            ).start()

        def taken(name, sems, like):
            if name in groups:
                pltpu.make_async_copy(like, like, sems.at[groups[name]]).wait()

        def first(buf, n):
            return buf.at[pl.ds(0, max(n, 1))]

        lane = lax.broadcasted_iota(jnp.int32, (1, 128), 1)
        row = jnp.zeros((1, 128), jnp.int32)
        for i, ref in ((0, first_ref), (1, second_ref)):
            for p in range(2):
                row = jnp.where(lane == 2 * i + p, ref[0, p], row)
        own_i[...] = row
        IX[0] = row
        IZ[0] = row
        loads[0].wait()
        GCA[0] = con_v[0:16, :]
        GCB[0] = con_v[16:32, :]
        xt[...] = jnp.zeros_like(xt)
        xr[...] = jnp.zeros_like(xr)
        loads[1].wait()
        xt[:, 0:64] = exc_v[...].astype(F32)
        xr[:, 0:NE] = xt[...].T[:, 0:NE]
        packed = xr[pl.ds(0, 8, stride=8), :]
        for k in range(1, 8):
            packed = packed + pltpu.roll(xr[pl.ds(k, 8, stride=8), :], NE * k, 1)
        GE[0] = packed.astype(BF16)
        loads[2].wait()
        GVA[0] = val_v[0:16, :]
        GVB[0] = val_v[16:32, :]
        pl.semaphore_wait(barrier, len(peers))

        for d in far_first(nx):
            send("ix", own_i, IX.at[d], at_x(d, core))
        for d in far_first(nz):
            send("iz", own_i, IZ.at[d], at_z(d, core))
        for d in far_first(nx):
            send("ca1", con_v.at[pl.ds(0, 16)], GCA.at[d], at_x(d, core))
        for d in far_first(nz):
            send("cb1", con_v.at[pl.ds(16, 16)], GCB.at[d], at_z(d, core))
        for d in far_first(nx):
            send("e1", GE.at[0], GE.at[d], at_x(d, core))
        for d in far_first(nx):
            send("va1", val_v.at[pl.ds(0, 16)], GVA.at[d], at_x(d, core))
        for d in far_first(nz):
            send("vb1", val_v.at[pl.ds(16, 16)], GVB.at[d], at_z(d, core))
        send("w", scr_ref, W.at[core], at_y(0, other))

        taken("ix", recv_sem, first(IX, nx - 1))
        ix_down = pltpu.make_async_copy(IX, SX, local_sem.at[0])
        ix_down.start()
        taken("iz", recv_sem, first(IZ, nz - 1))
        iz_down = pltpu.make_async_copy(IZ, SZ, local_sem.at[1])
        iz_down.start()

        def place(k, here, n, of):
            return lax.rem(here - of(k) + n, n)

        def kx_of(k):
            return lax.div(k, nz)

        def kz_of(k):
            return lax.rem(k, nz)

        iz_down.wait()
        ix_down.wait()
        from_x = {}
        from_z = {}
        for p in range(2):
            for r in range(2):
                for d in range(nz):
                    from_x[d, p, r] = place(SZ[(nz - d) % nz, 0, 2 * r + p], x, nx, kx_of)
                for d in range(nx):
                    from_z[d, p, r] = place(SX[(nx - d) % nx, 0, 2 * r + p], z, nz, kz_of)

        def hand_on(name, roles, held, packed, landed, where, n, at):
            order = far_first(n) + [0]
            for d in order:
                for p in range(2):
                    for r in roles:
                        packed[r, 2 * d + p] = held[where[d, p, r]]
            for r in roles:
                for d in order[:-1]:
                    for p in range(2):
                        send(f"{name}{r}", packed.at[r, 2 * d + p], landed[r].at[2 * d + core], at(d, p))
                send(f"{name}{r}", packed.at[r, other], landed[r].at[core], at(0, other))
                landed[r][core] = packed[r, core]

        taken("ca1", recv_sem, first(GCA, nx - 1))
        hand_on("ca2", (0,), GCA, PCA, RCA, from_x, nz, at_z)
        taken("cb1", recv_sem, first(GCB, nz - 1))
        hand_on("cb2", (0,), GCB, PCB, RCB, from_z, nx, at_x)
        hand_on("ca2", (1,), GCA, PCA, RCA, from_x, nz, at_z)
        hand_on("cb2", (1,), GCB, PCB, RCB, from_z, nx, at_x)
        taken("e1", recv_sem, first(GE, nx - 1))
        hand_on("e2", (0, 1), GE, PE, RE, from_x, nz, at_z)

        mine = []
        for ref in (first_ref, second_ref):
            k = ref[0, core]
            mine.append((place(k, z, nz, kz_of), place(k, x, nx, kx_of)))

        class Spread:
            def __init__(self, name, buf):
                self.name, self.buf = name, buf

            def begin(self):
                for d in [d for d in far_first(ny) if min(d, ny - d) <= 2]:
                    send(f"{self.name}{d}", self.buf(0), self.buf(d), at_y(d, core))

            def relay(self):
                if ny < 8:
                    return
                for d, step, half in ((2, 1, 0), (6, 7, 1)):
                    self.take(d)
                    at2, at1 = (2 * step) % ny, step
                    send(f"{self.name}4{half}", self.buf(d, half), self.buf(4, half), at_y(at2, core))
                    far = (d + step) % ny
                    send(f"{self.name}{far}", self.buf(d), self.buf(far), at_y(at1, core))

            def take(self, d, sems=recv_sem):
                if d == 4 and ny == 8:
                    for half in range(2):
                        taken(f"{self.name}4{half}", sems, self.buf(4, half))
                else:
                    taken(f"{self.name}{d}", sems, self.buf(d))

        def view_of(buf, r):
            def view(d, half=None):
                return buf.at[r, d] if half is None else buf.at[r, d, half]
            return view

        rings = [Spread("y0", view_of(CB, 0)), Spread("y1", view_of(CB, 1)), Spread("ye", view_of(EB, 0))]

        for r in range(2):
            taken(f"ca2{r}", recv_sem, first(RCA[r], 2 * nz - 1))
            for c in range(2):
                CB[r, 0, c, 0:16, :] = RCA[r][2 * mine[r][0] + c]
            taken(f"cb2{r}", recv_sem, first(RCB[r], 2 * nx - 1))
            for c in range(2):
                CB[r, 0, c, 16:32, :] = RCB[r][2 * mine[r][1] + c]
            rings[r].begin()
        taken("va1", recv_sem, first(GVA, nx - 1))
        hand_on("va2", (0, 1), GVA, PVA, RVA, from_x, nz, at_z)
        taken("vb1", recv_sem, first(GVB, nz - 1))
        hand_on("vb2", (0, 1), GVB, PVB, RVB, from_z, nx, at_x)
        for r in range(2):
            taken(f"e2{r}", recv_sem, first(RE[r], 2 * nz - 1))
            for c in range(2):
                EB[0, 0, c, r] = RE[r][2 * mine[r][0] + c]
        rings[2].begin()
        rings[0].relay()
        rings[1].relay()
        rings[2].relay()
        loads[3].wait()
        taken("w", recv_sem, W.at[0])

        def y_from(k):
            return lax.rem(y - k + ny, ny)

        def block(k):
            row = pl.multiple_of(y_from(k) * (2 * PT), 2 * PT)
            w = jnp.concatenate([W[0, pl.ds(row, 2 * PT), :], W[1, pl.ds(row, 2 * PT), :]], axis=1)
            c1 = jnp.concatenate([CB[0, k, 0], CB[0, k, 1]], axis=1).astype(F32)
            c2 = jnp.concatenate([CB[1, k, 0], CB[1, k, 1]], axis=1).astype(F32)
            for b in range(4):
                rho = jnp.concatenate(
                    [(c1[c : c + 1, :] * c2).astype(BF16) for c in range(8 * b, 8 * b + 8)], axis=0
                )
                part = jnp.dot(rho, w, preferred_element_type=F32)
                for lane in range(2):
                    piece = part[:, 128 * lane : 128 * lane + 128]
                    if k == 0:
                        S[lane, pl.ds(256 * b, 256), :] = piece
                    else:
                        S[lane, pl.ds(256 * b, 256), :] += piece

        block(0)
        near_first = sorted(range(1, ny), key=lambda d: (min(d, ny - d), d))
        for d in near_first:
            for r in range(2):
                if ny < 8 or d not in (2, 6):
                    rings[r].take(d)
            block(d)
        for r in range(2):
            taken(f"va2{r}", recv_sem, first(RVA[r], 2 * nz - 1))
            taken(f"vb2{r}", recv_sem, first(RVB[r], 2 * nx - 1))
        vals = []
        for r in range(2):
            halves = []
            for c in range(2):
                top = RVA[r][2 * mine[r][0] + c]
                low = RVB[r][2 * mine[r][1] + c]
                both = jnp.concatenate([top, low], axis=0)
                V32[r, c] = both.astype(F32)
                halves.append(both)
            vals.append(jnp.concatenate(halves, axis=1))
        for d in near_first:
            if ny < 8 or d not in (2, 6):
                rings[2].take(d)
        for k in range(ny):
            for c in range(2):
                row = pl.multiple_of((y_from(k) * 2 + c) * 8, 8)
                for role in (0, 1):
                    E32[role, pl.ds(row, 8), :] = EB[0, k, c, role].astype(F32)
        nw = 4 * ny
        for role, out in ((0, Y1), (1, Y2)):
            for q in range(4):
                eq = E32[role, pl.ds(q, nw, stride=4), :].astype(BF16)
                out[pl.ds(q * 128, 128), :] = lax.dot_general(
                    eq, vals[role][0:nw], (((0,), (0,)), ((), ())), preferred_element_type=F32
                )
        Zb[...] = jnp.zeros_like(Zb)

        def z_block(i, carry):
            for lane in range(2):
                cols = pl.ds(lane * 128, 128)
                y1 = [Y1[pl.ds(pl.multiple_of((i * 8 + c) * NE, NE), NE), cols] for c in range(8)]

                def over_d(d, acc):
                    at = pl.multiple_of(d * NE, NE)
                    y2 = Y2[pl.ds(at, NE), cols]
                    mirror = pl.multiple_of((d + 7 - 2 * lax.rem(d, 8)) * NE, NE)
                    new = []
                    terms = [Zb[pl.ds(mirror, NE), cols]]
                    for c in range(8):
                        s = S[lane, pl.ds((i * 8 + c) * NB + d, 1), :]
                        new.append(acc[c] + s * y2)
                        terms.append(s * y1[c])
                    while len(terms) > 1:
                        terms = [sum(terms[j : j + 2][1:], terms[j]) for j in range(0, len(terms), 2)]
                    Zb[pl.ds(mirror, NE), cols] = terms[0]
                    return tuple(new)

                zero = tuple(jnp.zeros((NE, 128), F32) for c in range(8))
                acc = lax.fori_loop(0, NB, over_d, zero, unroll=4)
                for c in range(8):
                    Zf[pl.ds(pl.multiple_of((i * 8 + 7 - c) * NE, NE), NE), cols] = acc[c]
            return carry

        lax.fori_loop(0, 4, z_block, 0)

        for fb, Z, role in ((0, Zf, 0), (1, Zb, 1)):
            v = jnp.concatenate(
                [
                    jnp.concatenate(
                        [V32[role, lane, pl.ds(i, 16, stride=2), :] for lane in range(2)], axis=1
                    )
                    for i in range(2)
                ],
                axis=0,
            ).astype(BF16)
            for h in range(4):
                f = lax.dot_general(
                    v, Z[pl.ds(h * 128, 128), :].astype(BF16), (((1,), (1,)), ((), ())),
                    preferred_element_type=F32,
                )
                for i in range(2):
                    T32[pl.ds(fb * 8 + h * 2 + i, 16, stride=16), :] = f[16 * i : 16 * i + 16, :]
        for s in range(n_scr):
            SB[s] = T32[pl.ds(16 * s, 16), :].astype(BF16)
        for d in far_first(ny) + [0]:
            for c in (core, other):
                to = lax.rem(y + d, ny) * 2 + c
                if d > 0 or c is other:
                    send("sum", SB.at[to], RB.at[core * ny + d], (g, to))
        RB[core * ny] = SB[sc]
        for name, like in (
            ("ix", first(IX, nx - 1)), ("iz", first(IZ, nz - 1)),
            ("ca1", first(GCA, nx - 1)), ("cb1", first(GCB, nz - 1)),
            ("e1", first(GE, nx - 1)),
            ("va1", first(GVA, nx - 1)), ("vb1", first(GVB, nz - 1)),
            ("w", W.at[0]),
            ("sum", first(RB, n_scr - 1)),
        ):
            taken(name, send_sem, like)
        for r in range(2):
            taken(f"ca2{r}", send_sem, first(RCA[r], 2 * nz - 1))
            taken(f"cb2{r}", send_sem, first(RCB[r], 2 * nx - 1))
            taken(f"e2{r}", send_sem, first(RE[r], 2 * nz - 1))
            taken(f"va2{r}", send_sem, first(RVA[r], 2 * nz - 1))
            taken(f"vb2{r}", send_sem, first(RVB[r], 2 * nx - 1))
        for spread in rings:
            for d in range(1, ny):
                spread.take(d, send_sem)
        taken("sum", recv_sem, first(RB, n_scr - 1))
        O32[...] = jnp.zeros_like(O32)
        for p in range(2):
            live = jnp.where(p < cnt_ref[0], 1.0, 0.0).astype(F32)
            tot = RB[p * ny].astype(F32)
            for d in range(1, ny):
                tot = tot + RB[p * ny + d].astype(F32)
            tot = tot * live
            for fb, out in ((0, fwd_ref), (1, back_ref)):
                for i in range(2):
                    for h in range(4):
                        r = fb * 8 + h * 2 + i
                        row = jnp.broadcast_to(tot[r : r + 1, :], (8, 128))
                        O32[pl.ds(i * 32 + h * 8, 8), :] = pltpu.roll(
                            pltpu.roll(row, NE, 1), 0, 1, stride=NE, stride_axis=0
                        )
                out[p] = O32[...].T[0:NE, 0:64]

    def run(wave_val, wave_con, excite, screening, pair_count, pair_kpoint, pair_partner):
        vmem = pl.BlockSpec(memory_space=pltpu.VMEM)
        smem = pl.BlockSpec(memory_space=pltpu.SMEM)
        hbm = pl.BlockSpec(memory_space=pl.ANY)
        n_mu = 2 * PT * ny
        shape = jax.ShapeDtypeStruct((2, NE, 64), F32)
        V = pltpu.VMEM
        fwd, back = pl.pallas_call(
            kernel,
            out_shape=(shape, shape),
            in_specs=[hbm, hbm, hbm, hbm, smem, smem, smem],
            out_specs=(vmem, vmem),
            scratch_shapes=[
                V((2, n_mu, PT), BF16),
                V((NB, PT), BF16), V((NB, PT), BF16), V((NE, 64), BF16),
                V((1, 128), jnp.int32), V((nx, 1, 128), jnp.int32), V((nz, 1, 128), jnp.int32),
                pltpu.SMEM((nx, 1, 128), jnp.int32), pltpu.SMEM((nz, 1, 128), jnp.int32),
                V((nx, 16, PT), BF16), V((nz, 16, PT), BF16),
                V((nx, 16, PT), BF16), V((nz, 16, PT), BF16), V((nx, 8, PT), BF16),
                V((2, 2 * nz, 16, PT), BF16), V((2, 2 * nx, 16, PT), BF16),
                V((2, 2 * nz, 16, PT), BF16), V((2, 2 * nx, 16, PT), BF16), V((2, 2 * nz, 8, PT), BF16),
                V((2 * nz, 16, PT), BF16), V((2 * nz, 16, PT), BF16),
                V((2 * nx, 16, PT), BF16), V((2 * nx, 16, PT), BF16),
                V((2 * nz, 16, PT), BF16), V((2 * nz, 16, PT), BF16),
                V((2 * nx, 16, PT), BF16), V((2 * nx, 16, PT), BF16),
                V((2 * nz, 8, PT), BF16), V((2 * nz, 8, PT), BF16),
                V((2, ny, 2, NB, PT), BF16), V((1, ny, 2, 2, 8, PT), BF16),
                V((16, 128), F32), V((128, 128), F32),
                V((2, NB * NB, PT), F32),
                V((2, 16 * ny, 128), F32),
                V((DE, 2 * PT), F32), V((DE, 2 * PT), F32),
                V((2, 2, NB, PT), F32),
                V((DE, 2 * PT), F32), V((DE, 2 * PT), F32),
                V((256, 128), F32), V((16, 16, 128), BF16), V((n_scr, 16, 128), BF16),
                V((128, 128), F32),
                pltpu.SemaphoreType.DMA((n_groups,)), pltpu.SemaphoreType.DMA((n_groups,)),
                pltpu.SemaphoreType.DMA((4,)),
            ],
            compiler_params=pltpu.CompilerParams(
                collective_id=0, has_side_effects=True, vmem_limit_bytes=60 * 1024 * 1024
            ),
        )(
            wave_val[0], wave_con[0], jnp.transpose(excite[0]), screening[0],
            pair_count, pair_kpoint, pair_partner,
        )
        return jnp.swapaxes(fwd, 1, 2)[None], jnp.swapaxes(back, 1, 2)[None]

    return run


def solution(mesh, sides=None):
    side = math.isqrt(mesh.shape["kgrp"])
    nx, nz = sides or (side, side)
    return jax.shard_map(
        build(nx, nz, mesh.shape["scr"] // 2),
        mesh=mesh,
        in_specs=(
            P("kgrp", None, "scr"),
            P("kgrp", None, "scr"),
            P("kgrp", "scr", None),
            P("kgrp", None, "scr"),
            P("kgrp"),
            P("kgrp", None),
            P("kgrp", None),
        ),
        out_specs=(P("kgrp", None, "scr", None), P("kgrp", None, "scr", None)),
        check_vma=False,
    )
```

```python
import math

import jax
import jax.numpy as jnp
from jax import lax
from jax.experimental import pallas as pl
from jax.experimental.pallas import tpu as pltpu
from jax.sharding import PartitionSpec as P

MESH = pl.DeviceIdType.MESH
BF16 = jnp.bfloat16
F32 = jnp.float32

NB = 32
NE = 16
PT = 128
DE = NB * NE


def build(nx, nz, ny):
    n_scr = 2 * ny
    n_groups = 34

    def kernel(
        val_ref, con_ref, exc_ref, scr_ref, cnt_ref, first_ref, second_ref,
        out_ref,
        W, con_v, val_v, exc_v, own_i, IX, IZ, SX, SZ,
        GCA, GCB, GVA, GVB, GE, PCA, PCB, PVA, PVB, PE, RCA0, RCA1, RCB0, RCB1, RVA0, RVA1, RVB0, RVB1, RE0, RE1,
        CB, EB, xt, xr, S, E32, Y1, Y2, V32, Zf, Zb, T32, SB, RB, O32,
        send_sem, recv_sem, local_sem,
    ):
        g = lax.axis_index("kgrp")
        sc = lax.axis_index("scr")
        x = lax.div(g, nz)
        z = lax.rem(g, nz)
        y = lax.div(sc, 2)
        core = lax.rem(sc, 2)
        other = 1 - core

        def at_x(d, c):
            return (lax.rem(x + d, nx) * nz + z, y * 2 + c)

        def at_z(d, c):
            return (x * nz + lax.rem(z + d, nz), y * 2 + c)

        def at_y(d, c):
            return (g, lax.rem(y + d, ny) * 2 + c)

        def far_first(n):
            return sorted(range(1, n), key=lambda d: -min(d, n - d))

        RCA, RCB, RVA, RVB, RE = (RCA0, RCA1), (RCB0, RCB1), (RVA0, RVA1), (RVB0, RVB1), (RE0, RE1)

        loads = [
            pltpu.make_async_copy(src, dst, local_sem.at[i])
            for i, (src, dst) in enumerate(
                ((con_ref, con_v), (exc_ref, exc_v), (val_ref, val_v), (scr_ref, W.at[core]))
            )
        ]
        for load in loads:
            load.start()
        peers = [at_x(d, c) for d in far_first(nx) for c in (core, other)]
        peers += [at_z(d, c) for d in far_first(nz) for c in (core, other)]
        peers += [at_y(d, core) for d in far_first(ny)] + [at_y(0, other)]
        barrier = pltpu.get_barrier_semaphore()
        for peer in peers:
            pl.semaphore_signal(barrier, inc=1, device_id=peer, device_id_type=MESH)

        groups = {}
        sent = {0: 0, 1: 0}

        def send(name, src, dst, to):
            k = groups.setdefault(name, len(groups))
            out = 0 if name == "w" else 1
            sent[out] += math.prod(src.shape) * jnp.dtype(src.dtype).itemsize
            pltpu.make_async_remote_copy(
                src_ref=src, dst_ref=dst, send_sem=send_sem.at[out], recv_sem=recv_sem.at[k],
                device_id=to, device_id_type=MESH,
            ).start()

        def taken(name, like):
            if name in groups:
                pltpu.make_async_copy(like, like, recv_sem.at[groups[name]]).wait()

        def first(buf, n):
            return buf.at[pl.ds(0, max(n, 1))]

        lane = lax.broadcasted_iota(jnp.int32, (1, 128), 1)
        row = jnp.zeros((1, 128), jnp.int32)
        for i, ref in ((0, first_ref), (1, second_ref)):
            for p in range(2):
                row = jnp.where(lane == 2 * i + p, ref[0, p], row)
        own_i[...] = row
        IX[0] = row
        IZ[0] = row
        loads[0].wait()
        GCA[0] = con_v[0:16, :]
        GCB[0] = con_v[16:32, :]
        xt[...] = jnp.zeros_like(xt)
        xr[...] = jnp.zeros_like(xr)
        loads[1].wait()
        xt[:, 0:64] = exc_v[...].astype(F32)
        xr[:, 0:NE] = xt[...].T[:, 0:NE]
        packed = xr[pl.ds(0, 8, stride=8), :]
        for k in range(1, 8):
            packed = packed + pltpu.roll(xr[pl.ds(k, 8, stride=8), :], NE * k, 1)
        GE[0] = packed.astype(BF16)
        loads[2].wait()
        GVA[0] = val_v[0:16, :]
        GVB[0] = val_v[16:32, :]
        pl.semaphore_wait(barrier, len(peers))

        for d in far_first(nx):
            send("ix", own_i, IX.at[d], at_x(d, core))
        for d in far_first(nz):
            send("iz", own_i, IZ.at[d], at_z(d, core))
        for d in far_first(nx):
            send("ca1", con_v.at[pl.ds(0, 16)], GCA.at[d], at_x(d, core))
        for d in far_first(nz):
            send("cb1", con_v.at[pl.ds(16, 16)], GCB.at[d], at_z(d, core))
        for d in far_first(nx):
            send("e1", GE.at[0], GE.at[d], at_x(d, core))
        for d in far_first(nx):
            send("va1", val_v.at[pl.ds(0, 16)], GVA.at[d], at_x(d, core))
        for d in far_first(nz):
            send("vb1", val_v.at[pl.ds(16, 16)], GVB.at[d], at_z(d, core))
        send("w", scr_ref, W.at[core], at_y(0, other))

        taken("ix", first(IX, nx - 1))
        ix_down = pltpu.make_async_copy(IX, SX, local_sem.at[0])
        ix_down.start()
        taken("iz", first(IZ, nz - 1))
        iz_down = pltpu.make_async_copy(IZ, SZ, local_sem.at[1])
        iz_down.start()

        def place(k, here, n, of):
            return lax.rem(here - of(k) + n, n)

        def kx_of(k):
            return lax.div(k, nz)

        def kz_of(k):
            return lax.rem(k, nz)

        iz_down.wait()
        ix_down.wait()
        from_x = {}
        from_z = {}
        for p in range(2):
            for r in range(2):
                for d in range(nz):
                    from_x[d, p, r] = place(SZ[(nz - d) % nz, 0, 2 * r + p], x, nx, kx_of)
                for d in range(nx):
                    from_z[d, p, r] = place(SX[(nx - d) % nx, 0, 2 * r + p], z, nz, kz_of)

        def hand_on(name, roles, held, packed, landed, where, n, at):
            order = far_first(n) + [0]
            for d in order:
                for p in range(2):
                    for r in roles:
                        packed[r, 2 * d + p] = held[where[d, p, r]]
            for r in roles:
                for d in order[:-1]:
                    for p in range(2):
                        send(f"{name}{r}", packed.at[r, 2 * d + p], landed[r].at[2 * d + core], at(d, p))
                send(f"{name}{r}", packed.at[r, other], landed[r].at[core], at(0, other))
                landed[r][core] = packed[r, core]

        taken("ca1", first(GCA, nx - 1))
        hand_on("ca2", (0,), GCA, PCA, RCA, from_x, nz, at_z)
        taken("cb1", first(GCB, nz - 1))
        hand_on("cb2", (0,), GCB, PCB, RCB, from_z, nx, at_x)
        hand_on("ca2", (1,), GCA, PCA, RCA, from_x, nz, at_z)
        hand_on("cb2", (1,), GCB, PCB, RCB, from_z, nx, at_x)
        taken("e1", first(GE, nx - 1))
        hand_on("e2", (0, 1), GE, PE, RE, from_x, nz, at_z)

        mine = []
        for ref in (first_ref, second_ref):
            k = ref[0, core]
            mine.append((place(k, z, nz, kz_of), place(k, x, nx, kx_of)))

        class Spread:
            def __init__(self, name, buf, parts):
                self.name, self.buf = name, buf
                self.group = {d: part for part in parts for d in part}

            def send(self, here, there, to, half=None):
                name = f"{self.name}{self.group[there][0]}"
                send(name, self.buf(here, half), self.buf(there, half), at_y(to, core))

            def begin(self):
                for d in [d for d in far_first(ny) if min(d, ny - d) <= 2]:
                    self.send(0, d, d)

            def relay(self):
                if ny < 8:
                    return
                for d, step, half in ((2, 1, 0), (6, 7, 1)):
                    self.take(d)
                    self.send(d, 4, (2 * step) % ny, half)
                    self.send(d, (d + step) % ny, step)

            def take(self, d):
                part = self.group[d]
                if d == part[0]:
                    taken(f"{self.name}{d}", self.buf(pl.ds(0, len(part))))

        def view_of(buf, r):
            def view(d, half=None):
                return buf.at[r, d] if half is None else buf.at[r, d, half]
            return view

        near_first = sorted(range(1, ny), key=lambda d: (min(d, ny - d), d))
        if ny == 8:
            parts = ((2,), (6,), (1, 7), (3,), (5,), (4,))
            parts_e = ((2,), (6,), (1, 7, 3, 5, 4))
        else:
            parts, parts_e = [(d,) for d in near_first], [tuple(near_first)]
        rings = [
            Spread("y0", view_of(CB, 0), parts),
            Spread("y1", view_of(CB, 1), parts),
            Spread("ye", view_of(EB, 0), parts_e),
        ]

        for r in range(2):
            taken(f"ca2{r}", first(RCA[r], 2 * nz - 1))
            for c in range(2):
                CB[r, 0, c, 0:16, :] = RCA[r][2 * mine[r][0] + c]
            taken(f"cb2{r}", first(RCB[r], 2 * nx - 1))
            for c in range(2):
                CB[r, 0, c, 16:32, :] = RCB[r][2 * mine[r][1] + c]
            rings[r].begin()
        taken("va1", first(GVA, nx - 1))
        hand_on("va2", (0, 1), GVA, PVA, RVA, from_x, nz, at_z)
        taken("vb1", first(GVB, nz - 1))
        hand_on("vb2", (0, 1), GVB, PVB, RVB, from_z, nx, at_x)
        for r in range(2):
            taken(f"e2{r}", first(RE[r], 2 * nz - 1))
            for c in range(2):
                EB[0, 0, c, r] = RE[r][2 * mine[r][0] + c]
        rings[2].begin()
        rings[0].relay()
        rings[1].relay()
        rings[2].relay()
        loads[3].wait()
        taken("w", W.at[0])

        def y_from(k):
            return lax.rem(y - k + ny, ny)

        def block(k):
            row = pl.multiple_of(y_from(k) * (2 * PT), 2 * PT)
            w = jnp.concatenate([W[0, pl.ds(row, 2 * PT), :], W[1, pl.ds(row, 2 * PT), :]], axis=1)
            c1 = jnp.concatenate([CB[0, k, 0], CB[0, k, 1]], axis=1).astype(F32)
            c2 = jnp.concatenate([CB[1, k, 0], CB[1, k, 1]], axis=1).astype(F32)
            for b in range(4):
                rho = jnp.concatenate(
                    [(c1[c : c + 1, :] * c2).astype(BF16) for c in range(8 * b, 8 * b + 8)], axis=0
                )
                part = jnp.dot(rho, w, preferred_element_type=F32)
                for lane in range(2):
                    piece = part[:, 128 * lane : 128 * lane + 128]
                    if k == 0:
                        S[lane, pl.ds(256 * b, 256), :] = piece
                    else:
                        S[lane, pl.ds(256 * b, 256), :] += piece

        block(0)
        for d in near_first:
            for r in range(2):
                if ny < 8 or d not in (2, 6):
                    rings[r].take(d)
            block(d)
        for r in range(2):
            taken(f"va2{r}", first(RVA[r], 2 * nz - 1))
            taken(f"vb2{r}", first(RVB[r], 2 * nx - 1))
        vals = []
        for r in range(2):
            halves = []
            for c in range(2):
                top = RVA[r][2 * mine[r][0] + c]
                low = RVB[r][2 * mine[r][1] + c]
                both = jnp.concatenate([top, low], axis=0)
                V32[r, c] = both.astype(F32)
                halves.append(both)
            vals.append(jnp.concatenate(halves, axis=1))
        for d in near_first:
            if ny < 8 or d not in (2, 6):
                rings[2].take(d)
        for k in range(ny):
            for c in range(2):
                row = pl.multiple_of((y_from(k) * 2 + c) * 8, 8)
                for role in (0, 1):
                    E32[role, pl.ds(row, 8), :] = EB[0, k, c, role].astype(F32)
        nw = 4 * ny
        for role, out in ((0, Y1), (1, Y2)):
            for q in range(4):
                eq = E32[role, pl.ds(q, nw, stride=4), :].astype(BF16)
                out[pl.ds(q * 128, 128), :] = lax.dot_general(
                    eq, vals[role][0:nw], (((0,), (0,)), ((), ())), preferred_element_type=F32
                )
        Zb[...] = jnp.zeros_like(Zb)

        def z_block(i, carry):
            for lane in range(2):
                cols = pl.ds(lane * 128, 128)
                y1 = [Y1[pl.ds(pl.multiple_of((i * 8 + c) * NE, NE), NE), cols] for c in range(8)]

                def over_d(d, acc):
                    at = pl.multiple_of(d * NE, NE)
                    y2 = Y2[pl.ds(at, NE), cols]
                    mirror = pl.multiple_of((d + 7 - 2 * lax.rem(d, 8)) * NE, NE)
                    new = []
                    terms = [Zb[pl.ds(mirror, NE), cols]]
                    for c in range(8):
                        s = S[lane, pl.ds((i * 8 + c) * NB + d, 1), :]
                        new.append(acc[c] + s * y2)
                        terms.append(s * y1[c])
                    while len(terms) > 1:
                        terms = [sum(terms[j : j + 2][1:], terms[j]) for j in range(0, len(terms), 2)]
                    Zb[pl.ds(mirror, NE), cols] = terms[0]
                    return tuple(new)

                zero = tuple(jnp.zeros((NE, 128), F32) for c in range(8))
                acc = lax.fori_loop(0, NB, over_d, zero, unroll=4)
                for c in range(8):
                    Zf[pl.ds(pl.multiple_of((i * 8 + 7 - c) * NE, NE), NE), cols] = acc[c]
            return carry

        lax.fori_loop(0, 4, z_block, 0)

        for fb, Z, role in ((0, Zf, 0), (1, Zb, 1)):
            v = jnp.concatenate(
                [
                    jnp.concatenate(
                        [V32[role, lane, pl.ds(i, 16, stride=2), :] for lane in range(2)], axis=1
                    )
                    for i in range(2)
                ],
                axis=0,
            ).astype(BF16)
            for h in range(4):
                f = lax.dot_general(
                    v, Z[pl.ds(h * 128, 128), :].astype(BF16), (((1,), (1,)), ((), ())),
                    preferred_element_type=F32,
                )
                for i in range(2):
                    T32[pl.ds(fb * 8 + h * 2 + i, 16, stride=16), :] = f[16 * i : 16 * i + 16, :]
        for s in range(n_scr):
            SB[s] = T32[pl.ds(16 * s, 16), :].astype(BF16)
        for d in far_first(ny) + [0]:
            for c in (core, other):
                to = lax.rem(y + d, ny) * 2 + c
                if d > 0 or c is other:
                    send("sum", SB.at[to], RB.at[core * ny + d], (g, to))
        RB[core * ny] = SB[sc]
        assert len(groups) <= n_groups
        for out in range(2):
            like = W.at[:, pl.ds(0, sent[out] // (4 * PT))]
            pltpu.make_async_copy(like, like, send_sem.at[out]).wait()
        taken("sum", first(RB, n_scr - 1))
        O32[...] = jnp.zeros_like(O32)
        for p in range(2):
            live = jnp.where(p < cnt_ref[0], 1.0, 0.0).astype(F32)
            tot = RB[p * ny].astype(F32)
            for d in range(1, ny):
                tot = tot + RB[p * ny + d].astype(F32)
            tot = tot * live
            for fb in range(2):
                for i in range(2):
                    for h in range(4):
                        r = fb * 8 + h * 2 + i
                        row = jnp.broadcast_to(tot[r : r + 1, :], (8, 128))
                        O32[pl.ds(i * 32 + h * 8, 8), :] = pltpu.roll(
                            pltpu.roll(row, NE, 1), 0, 1, stride=NE, stride_axis=0
                        )
                out_ref[fb, p] = O32[...].T[0:NE, 0:64]

    def run(wave_val, wave_con, excite, screening, pair_count, pair_kpoint, pair_partner):
        vmem = pl.BlockSpec(memory_space=pltpu.VMEM)
        smem = pl.BlockSpec(memory_space=pltpu.SMEM)
        hbm = pl.BlockSpec(memory_space=pl.ANY)
        n_mu = 2 * PT * ny
        shape = jax.ShapeDtypeStruct((2, 2, NE, 64), F32)
        V = pltpu.VMEM
        both = pl.pallas_call(
            kernel,
            out_shape=shape,
            in_specs=[hbm, hbm, hbm, hbm, smem, smem, smem],
            out_specs=vmem,
            scratch_shapes=[
                V((2, n_mu, PT), BF16),
                V((NB, PT), BF16), V((NB, PT), BF16), V((NE, 64), BF16),
                V((1, 128), jnp.int32), V((nx, 1, 128), jnp.int32), V((nz, 1, 128), jnp.int32),
                pltpu.SMEM((nx, 1, 128), jnp.int32), pltpu.SMEM((nz, 1, 128), jnp.int32),
                V((nx, 16, PT), BF16), V((nz, 16, PT), BF16),
                V((nx, 16, PT), BF16), V((nz, 16, PT), BF16), V((nx, 8, PT), BF16),
                V((2, 2 * nz, 16, PT), BF16), V((2, 2 * nx, 16, PT), BF16),
                V((2, 2 * nz, 16, PT), BF16), V((2, 2 * nx, 16, PT), BF16), V((2, 2 * nz, 8, PT), BF16),
                V((2 * nz, 16, PT), BF16), V((2 * nz, 16, PT), BF16),
                V((2 * nx, 16, PT), BF16), V((2 * nx, 16, PT), BF16),
                V((2 * nz, 16, PT), BF16), V((2 * nz, 16, PT), BF16),
                V((2 * nx, 16, PT), BF16), V((2 * nx, 16, PT), BF16),
                V((2 * nz, 8, PT), BF16), V((2 * nz, 8, PT), BF16),
                V((2, ny, 2, NB, PT), BF16), V((1, ny, 2, 2, 8, PT), BF16),
                V((16, 128), F32), V((128, 128), F32),
                V((2, NB * NB, PT), F32),
                V((2, 16 * ny, 128), F32),
                V((DE, 2 * PT), F32), V((DE, 2 * PT), F32),
                V((2, 2, NB, PT), F32),
                V((DE, 2 * PT), F32), V((DE, 2 * PT), F32),
                V((256, 128), F32), V((n_scr, 16, 128), BF16), V((n_scr, 16, 128), BF16),
                V((128, 128), F32),
                pltpu.SemaphoreType.DMA((2,)), pltpu.SemaphoreType.DMA((n_groups,)),
                pltpu.SemaphoreType.DMA((4,)),
            ],
            compiler_params=pltpu.CompilerParams(
                collective_id=0, has_side_effects=True, vmem_limit_bytes=60 * 1024 * 1024
            ),
        )(
            wave_val[0], wave_con[0], jnp.transpose(excite[0]), screening[0],
            pair_count, pair_kpoint, pair_partner,
        )
        both = jnp.swapaxes(both, 2, 3)
        return both[0][None], both[1][None]

    return run


def solution(mesh, sides=None):
    side = math.isqrt(mesh.shape["kgrp"])
    nx, nz = sides or (side, side)
    return jax.shard_map(
        build(nx, nz, mesh.shape["scr"] // 2),
        mesh=mesh,
        in_specs=(
            P("kgrp", None, "scr"),
            P("kgrp", None, "scr"),
            P("kgrp", "scr", None),
            P("kgrp", None, "scr"),
            P("kgrp"),
            P("kgrp", None),
            P("kgrp", None),
        ),
        out_specs=(P("kgrp", None, "scr", None), P("kgrp", None, "scr", None)),
        check_vma=False,
    )
```
